32 devices in a mesh: rep: 2 (over y), blk: 16 (over z, x, core).
Axes of the slice: x: 2, y: 2, z: 4, core: 2. Of those that a mesh axis runs over, the one named last changes fastest.
Arguments:
- a_blocks: float32 [16, 48, 256, 256], P('blk', 'rep'), may hold values from -0.375 to 0.375
- a_rows: int32 [16, 48], P('blk', 'rep'), may hold values from 0 to 31, as said below
- a_cols: int32 [16, 48], P('blk', 'rep'), may hold values from 0 to 31, as said below
- b_blocks: float32 [16, 6, 256, 256], P('blk'), may hold values from -6 to 6
- b_rows: int32 [16, 6], P('blk'), may hold values from 0 to 31, as said below
- b_cols: int32 [16, 6], P('blk'), may hold values from 0 to 31
- b_count: int32 [16], P('blk'), may hold values from 1 to 6, as said below
- c_rows: int32 [16, 16], P('blk'), may hold values from 0 to 31, as said below
- c_cols: int32 [16, 16], P('blk'), may hold values from 0 to 31
Outputs:
- iterate: float32 [16, 16, 256, 256], P('blk', 'rep')
The draws below stay inside these ranges and needn't reach their ends.
Inputs may be any that keep to these rules, and one draw needn't show every extreme that they name: `a_rows`: entry [d, g] lies in the block rows d * 2 to d * 2 + 1. `a_cols`: entry [d, r * 6 * 4 + k * 4 + m] (m < 4) lies in the block rows e * 2 to e * 2 + 1 with e = (d + (r - 1) * 6 + k) modulo the size of blk. `b_rows`: entry [e, q] lies in the block rows e * 2 to e * 2 + 1. `b_count`: equals 6 on at least one index. `c_rows`: entry [d, t] lies in the block rows d * 2 to d * 2 + 1.
All inputs are finite; a program needn't handle non-finite values.
Results may differ from the reference program's by a relative error of at most 0.0003.
Values sent between devices are 32-bit elements; how exact they have to be, the bound alone decides.
A program may use at most 128 MiB of HBM per device.

```python
import jax
import jax.numpy as jnp
from jax import lax

BLOCK = 256
RB_DEV = 2
STEPS = 6
PANEL = 6
A_SLOTS = 4
TARGETS = 16
N_REP = 2
N_BLK = 16


def pattern(key):
    subkeys = jax.random.split(jax.random.fold_in(key, 7171), 11)
    devices = jnp.arange(N_BLK, dtype=jnp.int32)[:, None]
    groups = jnp.arange(N_REP * STEPS * A_SLOTS, dtype=jnp.int32)[None, :] // A_SLOTS
    offset = groups - N_REP // 2 * STEPS
    shape_a = (N_BLK, N_REP * STEPS * A_SLOTS)
    a_rows = devices * RB_DEV + jax.random.randint(subkeys[0], shape_a, 0, RB_DEV, dtype=jnp.int32)
    owners = (devices + offset) % N_BLK
    a_cols = owners * RB_DEV + jax.random.randint(subkeys[1], shape_a, 0, RB_DEV, dtype=jnp.int32)
    shape_b = (N_BLK, PANEL)
    b_rows = devices * RB_DEV + jax.random.randint(subkeys[2], shape_b, 0, RB_DEV, dtype=jnp.int32)
    column_owner = (devices + jax.random.randint(subkeys[3], shape_b, 0, 2, dtype=jnp.int32)) % N_BLK
    b_cols = column_owner * RB_DEV + jax.random.randint(subkeys[4], shape_b, 0, RB_DEV, dtype=jnp.int32)
    first_count = jax.random.randint(subkeys[5], (N_BLK,), 1, PANEL + 1, dtype=jnp.int32)
    second_count = jax.random.randint(subkeys[6], (N_BLK,), 1, PANEL + 1, dtype=jnp.int32)
    fullest = jax.random.randint(subkeys[7], (), 0, N_BLK, dtype=jnp.int32)
    b_count = jnp.where(devices[:, 0] == fullest, PANEL, jnp.minimum(first_count, second_count)).astype(jnp.int32)
    shape_c = (N_BLK, TARGETS)
    reach = jax.random.randint(subkeys[8], shape_c, -(N_REP // 2) * STEPS, (N_REP - N_REP // 2) * STEPS + 1, dtype=jnp.int32)
    c_rows = devices * RB_DEV + jax.random.randint(subkeys[9], shape_c, 0, RB_DEV, dtype=jnp.int32)
    c_cols = (devices + reach) % N_BLK * RB_DEV + jax.random.randint(subkeys[10], shape_c, 0, RB_DEV, dtype=jnp.int32)
    return (a_rows, a_cols, b_rows, b_cols, b_count, c_rows, c_cols)


def draw_a_rows(key, part):
    return pattern(key)[0]


def draw_a_cols(key, part):
    return pattern(key)[1]


def draw_b_rows(key, part):
    return pattern(key)[2]


def draw_b_cols(key, part):
    return pattern(key)[3]


def draw_b_count(key, part):
    return pattern(key)[4]


def draw_c_rows(key, part):
    return pattern(key)[5]


def draw_c_cols(key, part):
    return pattern(key)[6]


def steps_of(rng, shape, pieces, least, top_value):
    level = 1.0
    for dim, parts in pieces:
        heights = jax.random.uniform(jax.random.fold_in(jax.random.fold_in(rng, 6), dim), (parts,), jnp.float32, least / len(pieces), top_value / len(pieces))
        level = level * jnp.repeat(jnp.exp(heights), shape[dim] // parts).reshape((-1,) + (1,) * (len(shape) - 1 - dim))
    return level


def scatter_about(key, shape, spread, bound, shards=(), held_as=jnp.bfloat16):
    drawn = spread * jax.random.normal(key, shape, jnp.float32)
    if shards:
        drawn = drawn * steps_of(key, shape, shards, -0.22, 0.18)
    return jnp.clip(drawn, -bound, bound).astype(held_as)


def setup_inputs(seed: int = 0) -> dict:
    splits = jax.random.split(jax.random.key(seed), 10)
    a_blocks = scatter_about(splits[0], (N_BLK, N_REP * STEPS * A_SLOTS, BLOCK, BLOCK), BLOCK ** -0.5, 0.375, ((0, 16), (1, 2)), jnp.float32)
    a_rows = draw_a_rows(jax.random.fold_in(splits[9], 71), 0)
    a_cols = draw_a_cols(jax.random.fold_in(splits[9], 71), 0)
    b_blocks = scatter_about(splits[3], (N_BLK, PANEL, BLOCK, BLOCK), 1.0, 6.0, ((0, 16),), jnp.float32)
    b_rows = draw_b_rows(jax.random.fold_in(splits[9], 71), 0)
    b_cols = draw_b_cols(jax.random.fold_in(splits[9], 71), 0)
    b_count = draw_b_count(jax.random.fold_in(splits[9], 71), 0)
    c_rows = draw_c_rows(jax.random.fold_in(splits[9], 71), 0)
    c_cols = draw_c_cols(jax.random.fold_in(splits[9], 71), 0)
    return dict(a_blocks=a_blocks, a_rows=a_rows, a_cols=a_cols, b_blocks=b_blocks, b_rows=b_rows, b_cols=b_cols, b_count=b_count, c_rows=c_rows, c_cols=c_cols)


def one_device(items, b_blocks, b_rows, b_cols, b_count):
    a_group, a_row, a_col, target_rows, target_cols = items
    owners = (a_col // RB_DEV).astype(jnp.int32)
    panels = jnp.take(b_blocks, owners, axis=0)
    panel_rows = jnp.take(b_rows, owners, axis=0)
    panel_cols = jnp.take(b_cols, owners, axis=0)
    counts = jnp.take(b_count, owners, axis=0)
    products = jnp.einsum("kij,kqjl->kqil", a_group, panels, precision=lax.Precision.HIGHEST)
    slot_index = jnp.arange(PANEL, dtype=jnp.int32)
    live = slot_index[None, :] < counts[:, None]
    weights = (a_row[None, :, None] == target_rows[:, None, None]) & (a_col[None, :, None] == panel_rows[None, :, :]) & (panel_cols[None, :, :] == target_cols[:, None, None]) & live[None, :, :]
    product = jnp.einsum("tkq,kqil->til", weights.astype(jnp.float32), products, precision=lax.Precision.HIGHEST)
    diagonal = (target_rows == target_cols).astype(jnp.float32)
    identity = jnp.eye(BLOCK, dtype=jnp.float32)
    return 1.5 * diagonal[:, None, None] * identity[None, :, :] - 0.5 * product


def reference(a_blocks, a_rows, a_cols, b_blocks, b_rows, b_cols, b_count, c_rows, c_cols):
    def apply(items):
        return one_device(items, b_blocks, b_rows, b_cols, b_count)

    return lax.map(apply, (a_blocks, a_rows, a_cols, c_rows, c_cols))
```

```python
import functools

import jax
import jax.numpy as jnp
from jax import lax
from jax.experimental import pallas as pl
from jax.experimental.pallas import tpu as pltpu
from jax.sharding import PartitionSpec as P

STEPS = 6
A_SLOTS = 4
ROWS_DEV = 2
LANES = 128
MESH = pl.DeviceIdType.MESH


def kernel(
    n,
    a_rows,
    a_cols,
    c_rows,
    c_cols,
    meta_ref,
    a_ref,
    b_ref,
    out_ref,
    panels,
    metas,
    metas_s,
    a_vmem,
    a_split,
    prods,
    acc,
    far,
    local_sem,
    z_send,
    z_recv,
    x_send,
    x_recv,
    f_send,
    f_recv,
    s_send,
    s_recv,
    y_send,
    y_recv,
    m_send,
    m_recv,
):
    rep = lax.axis_index("rep")
    me = lax.axis_index("blk")
    core = lax.rem(me, 2)
    odd = lax.rem(me // 2, 2)
    slots = panels.shape[1]
    halves = panels.shape[2]
    q_count = panels.shape[3]
    block = panels.shape[4]
    targets = acc.shape[1]
    keep = targets // 2
    ahead = lax.rem(me + 4, n)
    behind = lax.rem(me + n - 4, n)
    z_to = jnp.where(rep == 0, ahead, behind)
    x_to = me + 2 - 4 * odd
    s_to = me + 1 - 2 * core
    near = jnp.where(rep == 0, odd, 1 - odd)

    barrier = pltpu.get_barrier_semaphore()
    for other in (ahead, behind, x_to, s_to):
        pl.semaphore_signal(barrier, inc=1, device_id=(rep, other), device_id_type=MESH)
    pl.semaphore_signal(barrier, inc=1, device_id=(1 - rep, me), device_id_type=MESH)
    pl.semaphore_wait(barrier, 5)

    def remote(src, dst, send, recv, to, r=None):
        return pltpu.make_async_remote_copy(
            src_ref=src,
            dst_ref=dst,
            send_sem=send,
            recv_sem=recv,
            device_id=(rep if r is None else r, to),
            device_id_type=MESH,
        )

    def own(h, q):
        return b_ref.at[q, :, pl.ds(h * LANES, LANES)]

    def z_copy(h, q):
        return remote(own(h, q), panels.at[0, 2, h, q], z_send.at[h, q], z_recv.at[h, q], z_to)

    def x_own(h, q):
        return remote(own(h, q), panels.at[0, 1, h, q], x_send.at[h, q], x_recv.at[h, q], x_to)

    def x_pass(h, q):
        return remote(
            panels.at[0, 2, h, q], panels.at[0, 1, h, q], x_send.at[h, q], x_recv.at[h, q], x_to
        )

    def f_copy(h, q):
        return remote(
            panels.at[0, 1, h, q], panels.at[0, 3, h, q], f_send.at[h, q], f_recv.at[h, q], z_to
        )

    def s_copy(s, h):
        return remote(panels.at[0, s, h], panels.at[1, s, h], s_send.at[s, h], s_recv.at[s, h], s_to)

    def meta_copy(index, src, line, slot, to):
        return remote(src, metas.at[line, slot], m_send.at[index], m_recv.at[index], to)

    def y_copy(h):
        return remote(
            acc.at[h, pl.ds((1 - rep) * keep, keep)],
            far.at[h],
            y_send.at[h],
            y_recv.at[h],
            me,
            1 - rep,
        )

    def start_own(h):
        for q in range(q_count):
            z_copy(h, q).start()

        @pl.when(near == 0)
        def _():
            for q in range(q_count):
                x_own(h, q).start()

    m_z = meta_copy(0, meta_ref, 0, 2, z_to)
    m_x = meta_copy(1, meta_ref, 0, 1, x_to)
    m_xp = meta_copy(1, metas.at[0, 2], 0, 1, x_to)
    m_f = meta_copy(2, metas.at[0, 1], 0, 3, z_to)
    m_s = [meta_copy(3 + s, metas.at[0, s], 1, s, s_to) for s in range(slots)]
    m_s[0] = meta_copy(3, meta_ref, 1, 0, s_to)

    m_z.start()

    @pl.when(near == 0)
    def _():
        m_x.start()

    m_s[0].start()
    start_own(0)
    mine = [
        pltpu.make_async_copy(
            b_ref.at[:, :, pl.ds(h * LANES, LANES)], panels.at[0, 0, h], local_sem.at[h]
        )
        for h in range(halves)
    ]
    for copy in mine:
        copy.start()
    a_copy = pltpu.make_async_copy(a_ref, a_vmem, local_sem.at[halves])
    a_copy.start()
    m_own = pltpu.make_async_copy(meta_ref, metas.at[0, 0], local_sem.at[halves + 1])
    m_own.start()
    for h in range(halves):
        mine[h].wait()
        s_copy(0, h).start()
    m_own.wait()

    m_z.wait_recv()

    @pl.when(near == 1)
    def _():
        m_xp.start()

    m_s[2].start()
    m_x.wait_recv()
    m_f.start()
    m_s[1].start()

    a_copy.wait()
    tile = 64

    def split_a(index, carry):
        k = index // (block // tile)
        rows = pl.ds(pl.multiple_of(lax.rem(index, block // tile) * tile, tile), tile)
        owner = lax.rem(me + (rep - 1) * STEPS + k + n, n)
        parts = [a_vmem[k * A_SLOTS + m, rows, :] for m in range(A_SLOTS)]
        for i in range(ROWS_DEV):
            for j in range(ROWS_DEV):
                total = None
                for m in range(A_SLOTS):
                    g = k * A_SLOTS + m
                    match = (a_rows[0, g] == me * ROWS_DEV + i) & (
                        a_cols[0, g] == owner * ROWS_DEV + j
                    )
                    term = jnp.where(match, 1.0, 0.0).astype(jnp.float32) * parts[m]
                    total = term if total is None else total + term
                high = total.astype(jnp.bfloat16)
                low = (total - high.astype(jnp.float32)).astype(jnp.bfloat16)
                a_split[k, j, i, rows, pl.ds(0, block)] = high
                a_split[k, j, i, rows, pl.ds(block, block)] = low
                a_split[k, j, i, rows, pl.ds(2 * block, block)] = high
        return carry

    lax.fori_loop(0, STEPS * (block // tile), split_a, 0)

    def clear(index, carry):
        h = index // targets
        t = lax.rem(index, targets)
        acc[h, t] = jnp.zeros((block, LANES), jnp.float32)
        return carry

    lax.fori_loop(0, halves * targets, clear, 0)

    m_f.wait_recv()
    m_s[3].start()
    for s in range(slots):
        m_s[s].wait_recv()
    m_scalar = pltpu.make_async_copy(metas, metas_s, local_sem.at[halves + 2])
    m_scalar.start()
    m_scalar.wait()

    def compute(line, slot, h):
        back = STEPS - 2 * slot + line * (1 - 2 * core)
        forth = 2 * slot + line * (1 - 2 * core)
        k = jnp.where(rep == 0, back, forth)

        @pl.when((k >= 0) & (k < STEPS))
        def _():
            def multiply(q, carry):
                piece = panels[line, slot, h, q]
                high = piece.astype(jnp.bfloat16)
                low = (piece - high.astype(jnp.float32)).astype(jnp.bfloat16)
                stacked = jnp.concatenate([high, high, low], axis=0)
                j = lax.rem(metas_s[line, slot, 0, q], ROWS_DEV)
                left = a_split[k, j].reshape(ROWS_DEV * block, 3 * block)
                product = jnp.dot(left, stacked, preferred_element_type=jnp.float32)
                prods[q] = product.reshape(ROWS_DEV, block, LANES)
                return carry

            lax.fori_loop(0, q_count, multiply, 0)

            def collect(t, carry):
                i = lax.rem(c_rows[0, t], ROWS_DEV)
                total = acc[h, t]
                for q in range(q_count):
                    match = metas_s[line, slot, 1, q] == c_cols[0, t]
                    total = total + jnp.where(match, 1.0, 0.0).astype(jnp.float32) * prods[q, i]
                acc[h, t] = total
                return carry

            lax.fori_loop(0, targets, collect, 0)

    for h in range(halves):
        compute(0, 0, h)
        s_copy(0, h).wait_recv()
        compute(1, 0, h)
        for q in range(q_count):
            z_copy(h, q).wait_recv()

            @pl.when(near == 1)
            def _():
                x_pass(h, q).start()

            x_own(h, q).wait_recv()
            f_copy(h, q).start()
        s_copy(2, h).start()
        s_copy(1, h).start()
        if h + 1 < halves:
            start_own(h + 1)
        compute(0, 2, h)
        compute(0, 1, h)
        s_copy(2, h).wait_recv()
        compute(1, 2, h)
        s_copy(1, h).wait_recv()
        compute(1, 1, h)
        for q in range(q_count):
            f_copy(h, q).wait_recv()
        s_copy(3, h).start()
        compute(0, 3, h)
        s_copy(3, h).wait_recv()
        compute(1, 3, h)
        y_copy(h).start()

    for h in range(halves):
        y_copy(h).wait_recv()

        def finish(t, carry):
            out_ref[t, :, pl.ds(h * LANES, LANES)] = acc[h, rep * keep + t] + far[h, t]
            return carry

        lax.fori_loop(0, keep, finish, 0)

    for copy in [m_z, m_x, m_f] + m_s:
        copy.wait_send()
    for h in range(halves):
        y_copy(h).wait_send()
        for s in range(slots):
            s_copy(s, h).wait_send()
        for q in range(q_count):
            z_copy(h, q).wait_send()
            x_own(h, q).wait_send()
            f_copy(h, q).wait_send()


def local(n, a_blocks, a_rows, a_cols, b_blocks, b_rows, b_cols, b_count, c_rows, c_cols):
    replica = lax.axis_index("rep")
    q_count, block = b_blocks.shape[1], b_blocks.shape[-1]
    a_slots = a_blocks.shape[1]
    targets = c_rows.shape[1]
    half = targets // lax.axis_size("rep")
    halves = block // LANES
    slots = STEPS // 2 + 1
    live = jnp.arange(q_count, dtype=jnp.int32) < b_count[0]
    cols = jnp.where(live, b_cols[0], -1)
    meta = jnp.pad(jnp.stack([b_rows[0], cols]), ((0, 6), (0, LANES - q_count)))
    smem = pl.BlockSpec(memory_space=pltpu.SMEM)
    vmem = pl.BlockSpec(memory_space=pltpu.VMEM)
    hbm = pl.BlockSpec(memory_space=pl.ANY)
    dma = pltpu.SemaphoreType.DMA
    summed = pl.pallas_call(
        functools.partial(kernel, n),
        out_shape=jax.ShapeDtypeStruct((half, block, block), jnp.float32),
        in_specs=[smem] * 4 + [vmem, hbm, hbm],
        out_specs=vmem,
        scratch_shapes=[
            pltpu.VMEM((2, slots, halves, q_count, block, LANES), jnp.float32),
            pltpu.VMEM((2, slots, 8, LANES), jnp.int32),
            pltpu.SMEM((2, slots, 8, LANES), jnp.int32),
            pltpu.VMEM((a_slots, block, block), jnp.float32),
            pltpu.VMEM((STEPS, ROWS_DEV, ROWS_DEV, block, 3 * block), jnp.bfloat16),
            pltpu.VMEM((q_count, ROWS_DEV, block, LANES), jnp.float32),
            pltpu.VMEM((halves, targets, block, LANES), jnp.float32),
            pltpu.VMEM((halves, half, block, LANES), jnp.float32),
            dma((halves + 3,)),
            dma((halves, q_count)),
            dma((halves, q_count)),
            dma((halves, q_count)),
            dma((halves, q_count)),
            dma((halves, q_count)),
            dma((halves, q_count)),
            dma((slots, halves)),
            dma((slots, halves)),
            dma((halves,)),
            dma((halves,)),
            dma((3 + slots,)),
            dma((3 + slots,)),
        ],
        compiler_params=pltpu.CompilerParams(
            collective_id=0, has_side_effects=True, vmem_limit_bytes=60 * 1024 * 1024
        ),
    )(a_rows, a_cols, c_rows, c_cols, meta, a_blocks[0], b_blocks[0])
    rows_half = lax.dynamic_slice_in_dim(c_rows[0], replica * half, half)
    cols_half = lax.dynamic_slice_in_dim(c_cols[0], replica * half, half)
    diagonal = (rows_half == cols_half).astype(jnp.float32)
    identity = jnp.eye(block, dtype=jnp.float32)
    result = 1.5 * diagonal[:, None, None] * identity[None, :, :] - 0.5 * summed
    return result[None]


def solution(mesh):
    return jax.shard_map(
        functools.partial(local, mesh.shape["blk"]),
        mesh=mesh,
        in_specs=(
            P("blk", "rep", None, None),
            P("blk", "rep"),
            P("blk", "rep"),
            P("blk", None, None, None),
            P("blk", None),
            P("blk", None),
            P("blk"),
            P("blk", None),
            P("blk", None),
        ),
        out_specs=P("blk", "rep", None, None),
        check_vma=False,
    )
```

```python
import functools

import jax
import jax.numpy as jnp
from jax import lax
from jax.experimental import pallas as pl
from jax.experimental.pallas import tpu as pltpu
from jax.sharding import PartitionSpec as P

STEPS = 6
A_SLOTS = 4
ROWS_DEV = 2
LANES = 128
MESH = pl.DeviceIdType.MESH


def kernel(
    n,
    a_rows,
    a_cols,
    c_rows,
    c_cols,
    b_rows,
    b_cols,
    b_count,
    a_ref,
    b_ref,
    out_ref,
    panels,
    detour,
    metas,
    metas_s,
    a_vmem,
    a_split,
    prods,
    acc,
    far,
    local_sem,
    z_send,
    z_recv,
    x_send,
    x_recv,
    f_send,
    f_recv,
    s_send,
    s_recv,
    p_send,
    d_recv,
    t_send,
    t_recv,
    y_send,
    y_recv,
    m_send,
    m_recv,
):
    rep = lax.axis_index("rep")
    me = lax.axis_index("blk")
    core = lax.rem(me, 2)
    odd = lax.rem(me // 2, 2)
    slots = panels.shape[1]
    halves = panels.shape[2]
    q_count = panels.shape[3]
    block = panels.shape[4]
    targets = acc.shape[1]
    keep = targets // 2
    ahead = lax.rem(me + 4, n)
    behind = lax.rem(me + n - 4, n)
    z_to = jnp.where(rep == 0, ahead, behind)
    x_to = me + 2 - 4 * odd
    s_to = me + 1 - 2 * core
    near = jnp.where(rep == 0, odd, 1 - odd)

    sub = lax.broadcasted_iota(jnp.int32, (8, LANES), 0)
    lane = lax.broadcasted_iota(jnp.int32, (8, LANES), 1)
    meta = jnp.zeros((8, LANES), jnp.int32)
    for q in range(q_count):
        col = jnp.where(q < b_count[0], b_cols[0, q], -1)
        meta = jnp.where((sub == 0) & (lane == q), b_rows[0, q], meta)
        meta = jnp.where((sub == 1) & (lane == q), col, meta)
    metas[0, 0] = meta

    barrier = pltpu.get_barrier_semaphore()
    for other in (ahead, behind, x_to, s_to):
        pl.semaphore_signal(barrier, inc=1, device_id=(rep, other), device_id_type=MESH)
    pl.semaphore_signal(barrier, inc=1, device_id=(1 - rep, me), device_id_type=MESH)
    pl.semaphore_wait(barrier, 5)

    def remote(src, dst, send, recv, to, r=None):
        return pltpu.make_async_remote_copy(
            src_ref=src,
            dst_ref=dst,
            send_sem=send,
            recv_sem=recv,
            device_id=(rep if r is None else r, to),
            device_id_type=MESH,
        )

    def own(h, q):
        return b_ref.at[q, :, pl.ds(h * LANES, LANES)]

    def z_copy(h, q):
        return remote(own(h, q), panels.at[0, 2, h, q], z_send.at[h, q], z_recv.at[h, q], z_to)

    def x_own(h, q):
        return remote(own(h, q), panels.at[0, 1, h, q], x_send.at[h, q], x_recv.at[h, q], x_to)

    def x_pass(h, q):
        return remote(
            panels.at[0, 2, h, q], panels.at[0, 1, h, q], x_send.at[h, q], x_recv.at[h, q], x_to
        )

    def f_copy(h, q):
        return remote(
            panels.at[0, 1, h, q], panels.at[0, 3, h, q], f_send.at[h, q], f_recv.at[h, q], z_to
        )

    def p_copy(h, q):
        return remote(
            panels.at[0, 2, h, q], panels.at[0, 3, h, q], p_send.at[h, q], f_recv.at[h, q], x_to
        )

    def d_copy(h, q):
        return remote(
            panels.at[0, 2, h, q], detour.at[h, q], f_send.at[h, q], d_recv.at[h, q], z_to
        )

    def dp_copy(h, q):
        return remote(
            detour.at[h, q], panels.at[0, 3, h, q], p_send.at[h, q], f_recv.at[h, q], x_to
        )

    def t_copy(h, q):
        return remote(
            panels.at[0, 3, h, q], panels.at[1, 3, h, q], t_send.at[h, q], t_recv.at[h, q], s_to
        )

    def s_copy(s, h):
        return remote(panels.at[0, s, h], panels.at[1, s, h], s_send.at[s, h], s_recv.at[s, h], s_to)

    def meta_copy(index, src, line, slot, to):
        return remote(src, metas.at[line, slot], m_send.at[index], m_recv.at[index], to)

    def y_copy(h, u):
        return remote(
            acc.at[h, (1 - rep) * keep + u],
            far.at[h, u],
            y_send.at[h, u],
            y_recv.at[h, u],
            me,
            1 - rep,
        )

    def start_own(h):
        for q in range(q_count):
            z_copy(h, q).start()

        @pl.when(near == 0)
        def _():
            for q in range(q_count):
                x_own(h, q).start()

    m_z = meta_copy(0, metas.at[0, 0], 0, 2, z_to)
    m_x = meta_copy(1, metas.at[0, 0], 0, 1, x_to)
    m_xp = meta_copy(1, metas.at[0, 2], 0, 1, x_to)
    m_f = meta_copy(2, metas.at[0, 1], 0, 3, z_to)
    m_s = [meta_copy(3 + s, metas.at[0, s], 1, s, s_to) for s in range(slots)]

    m_z.start()

    @pl.when(near == 0)
    def _():
        m_x.start()

    m_s[0].start()
    start_own(0)
    mine = [
        pltpu.make_async_copy(
            b_ref.at[:, :, pl.ds(h * LANES, LANES)], panels.at[0, 0, h], local_sem.at[h]
        )
        for h in range(halves)
    ]
    for copy in mine:
        copy.start()
    a_copy = pltpu.make_async_copy(a_ref, a_vmem, local_sem.at[halves])
    a_copy.start()
    for h in range(halves):
        mine[h].wait()
        s_copy(0, h).start()

    m_z.wait_recv()

    @pl.when(near == 1)
    def _():
        m_xp.start()

    m_s[2].start()
    m_x.wait_recv()
    m_f.start()
    m_s[1].start()

    a_copy.wait()
    tile = 64

    def split_a(k, index, carry):
        rows = pl.ds(pl.multiple_of(index * tile, tile), tile)
        owner = lax.rem(me + (rep - 1) * STEPS + k + n, n)
        parts = [a_vmem[k * A_SLOTS + m, rows, :] for m in range(A_SLOTS)]
        for i in range(ROWS_DEV):
            for j in range(ROWS_DEV):
                total = None
                for m in range(A_SLOTS):
                    g = k * A_SLOTS + m
                    match = (a_rows[0, g] == me * ROWS_DEV + i) & (
                        a_cols[0, g] == owner * ROWS_DEV + j
                    )
                    term = jnp.where(match, 1.0, 0.0).astype(jnp.float32) * parts[m]
                    total = term if total is None else total + term
                high = total.astype(jnp.bfloat16)
                low = (total - high.astype(jnp.float32)).astype(jnp.bfloat16)
                a_split[k, j, i, rows, pl.ds(0, block)] = high
                a_split[k, j, i, rows, pl.ds(block, block)] = low
                a_split[k, j, i, rows, pl.ds(2 * block, block)] = high
        return carry

    for k in range(STEPS):
        lax.fori_loop(0, block // tile, functools.partial(split_a, k), 0)

    def clear(index, carry):
        h = index // targets
        t = lax.rem(index, targets)
        acc[h, t] = jnp.zeros((block, LANES), jnp.float32)
        return carry

    lax.fori_loop(0, halves * targets, clear, 0)

    m_f.wait_recv()
    m_s[3].start()
    for s in range(slots):
        m_s[s].wait_recv()
    m_scalar = pltpu.make_async_copy(metas, metas_s, local_sem.at[halves + 1])
    m_scalar.start()
    m_scalar.wait()

    def step_of(line, slot):
        back = STEPS - 2 * slot + line * (1 - 2 * core)
        forth = 2 * slot + line * (1 - 2 * core)
        k = jnp.where(rep == 0, back, forth)
        return k, (k >= 0) & (k < STEPS)

    def multiply(line, slot, h, k, into, q):
        piece = panels[line, slot, h, q]
        high = piece.astype(jnp.bfloat16)
        low = (piece - high.astype(jnp.float32)).astype(jnp.bfloat16)
        stacked = jnp.concatenate([high, high, low], axis=0)
        j = lax.rem(metas_s[line, slot, 0, q], ROWS_DEV)
        left = a_split[k, j].reshape(ROWS_DEV * block, 3 * block)
        product = jnp.dot(left, stacked, preferred_element_type=jnp.float32)
        prods[into, q] = product.reshape(ROWS_DEV, block, LANES)

    def multiply_if(line, slot, h, into, q):
        k, needed = step_of(line, slot)

        @pl.when(needed)
        def _():
            multiply(line, slot, h, k, into, q)

    def collect(line, slot, h, into, t):
        i = lax.rem(c_rows[0, t], ROWS_DEV)
        total = acc[h, t]
        for q in range(q_count):
            match = metas_s[line, slot, 1, q] == c_cols[0, t]
            total = total + jnp.where(match, 1.0, 0.0).astype(jnp.float32) * prods[into, q, i]
        acc[h, t] = total

    def collect_all(line, slot, h, into):
        k, needed = step_of(line, slot)

        @pl.when(needed)
        def _():
            def body(t, carry):
                collect(line, slot, h, into, t)
                return carry

            lax.fori_loop(0, targets, body, 0)

    def compute(line, slot, h):
        k, needed = step_of(line, slot)

        @pl.when(needed)
        def _():
            def body(q, carry):
                multiply(line, slot, h, k, 0, q)
                return carry

            lax.fori_loop(0, q_count, body, 0)

        collect_all(line, slot, h, 0)

    few = q_count // 3
    many = 2 * few

    for h in range(halves):
        if h > 0:
            compute(0, 0, h)
            s_copy(0, h).wait_recv()
            compute(1, 0, h)
        for q in range(q_count):
            z_copy(h, q).wait_recv()

            @pl.when(near == 1)
            def _():
                x_pass(h, q).start()
                if q < few:
                    d_copy(h, q).start()

            if q < many:

                @pl.when(near == 0)
                def _():
                    p_copy(h, q).start()

            multiply_if(0, 2, h, 0, q)
            x_own(h, q).wait_recv()
            if q >= many:
                f_copy(h, q).start()
            elif q >= few:

                @pl.when(near == 0)
                def _():
                    f_copy(h, q).start()

            multiply_if(0, 1, h, 1, q)
        s_copy(2, h).start()
        s_copy(1, h).start()
        if h + 1 < halves:
            start_own(h + 1)
        collect_all(0, 2, h, 0)
        collect_all(0, 1, h, 1)
        s_copy(2, h).wait_recv()
        compute(1, 2, h)

        @pl.when(near == 1)
        def _():
            for q in range(few):
                d_copy(h, q).wait_recv()
                dp_copy(h, q).start()

        s_copy(1, h).wait_recv()
        compute(1, 1, h)
        if h == 0:
            compute(0, 0, h)
            s_copy(0, h).wait_recv()
            compute(1, 0, h)
        order = list(range(few, many)) + list(range(few)) + list(range(many, q_count))
        previous = None
        for q in order:
            f_copy(h, q).wait_recv()
            t_copy(h, q).start()
            multiply_if(0, 3, h, 0, q)
            if previous is not None:
                t_copy(h, previous).wait_recv()
                multiply_if(1, 3, h, 1, previous)
            previous = q
        t_copy(h, previous).wait_recv()
        multiply_if(1, 3, h, 1, previous)

        def last(base, t):
            for line in range(2):
                k, needed = step_of(line, 3)

                @pl.when(needed)
                def _():
                    collect(line, 3, h, line, base + t)

        def theirs(u, carry):
            last((1 - rep) * keep, u)

            @pl.when(u > 0)
            def _():
                y_copy(h, u - 1).start()

            return carry

        def ours(u, carry):
            last(rep * keep, u)
            return carry

        lax.fori_loop(0, keep, theirs, 0)
        y_copy(h, keep - 1).start()
        lax.fori_loop(0, keep, ours, 0)

    for h in range(halves):

        def finish(u, carry):
            y_copy(h, u).wait_recv()
            out_ref[u, :, pl.ds(h * LANES, LANES)] = acc[h, rep * keep + u] + far[h, u]
            return carry

        lax.fori_loop(0, keep, finish, 0)

    for copy in [m_z, m_x, m_f] + m_s:
        copy.wait_send()
    for h in range(halves):
        for u in range(keep):
            y_copy(h, u).wait_send()
        for s in range(slots - 1):
            s_copy(s, h).wait_send()
        for q in range(q_count):
            z_copy(h, q).wait_send()
            x_own(h, q).wait_send()
            t_copy(h, q).wait_send()
            if q < few:
                p_copy(h, q).wait_send()

                @pl.when(near == 1)
                def _():
                    d_copy(h, q).wait_send()

            elif q < many:

                @pl.when(near == 0)
                def _():
                    p_copy(h, q).wait_send()
                    f_copy(h, q).wait_send()

            else:
                f_copy(h, q).wait_send()


def local(n, a_blocks, a_rows, a_cols, b_blocks, b_rows, b_cols, b_count, c_rows, c_cols):
    replica = lax.axis_index("rep")
    q_count, block = b_blocks.shape[1], b_blocks.shape[-1]
    a_slots = a_blocks.shape[1]
    targets = c_rows.shape[1]
    half = targets // lax.axis_size("rep")
    halves = block // LANES
    slots = STEPS // 2 + 1
    smem = pl.BlockSpec(memory_space=pltpu.SMEM)
    vmem = pl.BlockSpec(memory_space=pltpu.VMEM)
    hbm = pl.BlockSpec(memory_space=pl.ANY)
    dma = pltpu.SemaphoreType.DMA
    summed = pl.pallas_call(
        functools.partial(kernel, n),
        out_shape=jax.ShapeDtypeStruct((half, block, block), jnp.float32),
        in_specs=[smem] * 7 + [hbm, hbm],
        out_specs=vmem,
        scratch_shapes=[
            pltpu.VMEM((2, slots, halves, q_count, block, LANES), jnp.float32),
            pltpu.VMEM((halves, q_count // 3, block, LANES), jnp.float32),
            pltpu.VMEM((2, slots, 8, LANES), jnp.int32),
            pltpu.SMEM((2, slots, 8, LANES), jnp.int32),
            pltpu.VMEM((a_slots, block, block), jnp.float32),
            pltpu.VMEM((STEPS, ROWS_DEV, ROWS_DEV, block, 3 * block), jnp.bfloat16),
            pltpu.VMEM((2, q_count, ROWS_DEV, block, LANES), jnp.float32),
            pltpu.VMEM((halves, targets, block, LANES), jnp.float32),
            pltpu.VMEM((halves, half, block, LANES), jnp.float32),
            dma((halves + 2,)),
            dma((halves, q_count)),
            dma((halves, q_count)),
            dma((halves, q_count)),
            dma((halves, q_count)),
            dma((halves, q_count)),
            dma((halves, q_count)),
            dma((slots, halves)),
            dma((slots, halves)),
            dma((halves, q_count)),
            dma((halves, q_count)),
            dma((halves, q_count)),
            dma((halves, q_count)),
            dma((halves, half)),
            dma((halves, half)),
            dma((3 + slots,)),
            dma((3 + slots,)),
        ],
        compiler_params=pltpu.CompilerParams(
            collective_id=0, has_side_effects=True, vmem_limit_bytes=60 * 1024 * 1024
        ),
    )(a_rows, a_cols, c_rows, c_cols, b_rows, b_cols, b_count, a_blocks[0], b_blocks[0])
    rows_half = lax.dynamic_slice_in_dim(c_rows[0], replica * half, half)
    cols_half = lax.dynamic_slice_in_dim(c_cols[0], replica * half, half)
    diagonal = (rows_half == cols_half).astype(jnp.float32)
    identity = jnp.eye(block, dtype=jnp.float32)
    result = 1.5 * diagonal[:, None, None] * identity[None, :, :] - 0.5 * summed
    return result[None]


def solution(mesh):
    return jax.shard_map(
        functools.partial(local, mesh.shape["blk"]),
        mesh=mesh,
        in_specs=(
            P("blk", "rep", None, None),
            P("blk", "rep"),
            P("blk", "rep"),
            P("blk", None, None, None),
            P("blk", None),
            P("blk", None),
            P("blk"),
            P("blk", None),
            P("blk", None),
        ),
        out_specs=P("blk", "rep", None, None),
        check_vma=False,
    )
```

```python
import functools

import jax
import jax.numpy as jnp
from jax import lax
from jax.experimental import pallas as pl
from jax.experimental.pallas import tpu as pltpu
from jax.sharding import PartitionSpec as P

STEPS = 6
A_SLOTS = 4
ROWS_DEV = 2
LANES = 128
MESH = pl.DeviceIdType.MESH


def kernel(
    n,
    a_rows,
    a_cols,
    c_rows,
    c_cols,
    b_rows,
    b_cols,
    b_count,
    a_ref,
    b_ref,
    out_ref,
    panels,
    detour,
    metas,
    metas_s,
    a_vmem,
    a_split,
    prods,
    acc,
    far,
    local_sem,
    z_send,
    z_recv,
    x_send,
    x_recv,
    f_send,
    f_recv,
    s_send,
    s_recv,
    p_send,
    d_recv,
    t_send,
    t_recv,
    y_send,
    y_recv,
    m_send,
    m_recv,
):
    rep = lax.axis_index("rep")
    me = lax.axis_index("blk")
    core = lax.rem(me, 2)
    odd = lax.rem(me // 2, 2)
    slots = panels.shape[1]
    halves = panels.shape[2]
    q_count = panels.shape[3]
    block = panels.shape[4]
    targets = acc.shape[1]
    keep = targets // 2
    ahead = lax.rem(me + 4, n)
    behind = lax.rem(me + n - 4, n)
    z_to = jnp.where(rep == 0, ahead, behind)
    x_to = me + 2 - 4 * odd
    s_to = me + 1 - 2 * core
    near = jnp.where(rep == 0, odd, 1 - odd)

    sub = lax.broadcasted_iota(jnp.int32, (8, LANES), 0)
    lane = lax.broadcasted_iota(jnp.int32, (8, LANES), 1)
    meta = jnp.zeros((8, LANES), jnp.int32)
    for q in range(q_count):
        col = jnp.where(q < b_count[0], b_cols[0, q], -1)
        meta = jnp.where((sub == 0) & (lane == q), b_rows[0, q], meta)
        meta = jnp.where((sub == 1) & (lane == q), col, meta)
    metas[0, 0] = meta

    barrier = pltpu.get_barrier_semaphore()
    for other in (ahead, behind, x_to, s_to):
        pl.semaphore_signal(barrier, inc=1, device_id=(rep, other), device_id_type=MESH)
    pl.semaphore_signal(barrier, inc=1, device_id=(1 - rep, me), device_id_type=MESH)
    pl.semaphore_wait(barrier, 5)

    def remote(src, dst, send, recv, to, r=None):
        return pltpu.make_async_remote_copy(
            src_ref=src,
            dst_ref=dst,
            send_sem=send,
            recv_sem=recv,
            device_id=(rep if r is None else r, to),
            device_id_type=MESH,
        )

    def own(h, q):
        return b_ref.at[q, :, pl.ds(h * LANES, LANES)]

    def z_copy(h, q):
        return remote(own(h, q), panels.at[0, 2, h, q], z_send.at[h, q], z_recv.at[h, q], z_to)

    def x_own(h, q):
        return remote(own(h, q), panels.at[0, 1, h, q], x_send.at[h, q], x_recv.at[h, q], x_to)

    def x_pass(h, q):
        return remote(
            panels.at[0, 2, h, q], panels.at[0, 1, h, q], x_send.at[h, q], x_recv.at[h, q], x_to
        )

    def f_copy(h, q):
        return remote(
            panels.at[0, 1, h, q], panels.at[0, 3, h, q], f_send.at[h, q], f_recv.at[h, q], z_to
        )

    def p_copy(h, q):
        return remote(
            panels.at[0, 2, h, q], panels.at[0, 3, h, q], p_send.at[h, q], f_recv.at[h, q], x_to
        )

    def d_copy(h, q):
        return remote(
            panels.at[0, 2, h, q], detour.at[h, q], f_send.at[h, q], d_recv.at[h, q], z_to
        )

    def dp_copy(h, q):
        return remote(
            detour.at[h, q], panels.at[0, 3, h, q], p_send.at[h, q], f_recv.at[h, q], x_to
        )

    def t_copy(h, q):
        return remote(
            panels.at[0, 3, h, q], panels.at[1, 3, h, q], t_send.at[h, q], t_recv.at[h, q], s_to
        )

    def s_copy(s, h):
        return remote(panels.at[0, s, h], panels.at[1, s, h], s_send.at[s, h], s_recv.at[s, h], s_to)

    def meta_copy(index, src, line, slot, to):
        return remote(src, metas.at[line, slot], m_send.at[index], m_recv.at[index], to)

    def y_copy(h, u):
        return remote(
            acc.at[h, (1 - rep) * keep + u],
            far.at[h, u],
            y_send.at[h, u],
            y_recv.at[h, u],
            me,
            1 - rep,
        )

    def start_own(h):
        for q in range(q_count):
            z_copy(h, q).start()

        @pl.when(near == 0)
        def _():
            for q in range(q_count):
                x_own(h, q).start()

    m_z = meta_copy(0, metas.at[0, 0], 0, 2, z_to)
    m_x = meta_copy(1, metas.at[0, 0], 0, 1, x_to)
    m_xp = meta_copy(1, metas.at[0, 2], 0, 1, x_to)
    m_f = meta_copy(2, metas.at[0, 1], 0, 3, z_to)
    m_s = [meta_copy(3 + s, metas.at[0, s], 1, s, s_to) for s in range(slots)]

    m_z.start()

    @pl.when(near == 0)
    def _():
        m_x.start()

    m_s[0].start()
    start_own(0)
    mine = [
        pltpu.make_async_copy(
            b_ref.at[:, :, pl.ds(h * LANES, LANES)], panels.at[0, 0, h], local_sem.at[h]
        )
        for h in range(halves)
    ]
    for copy in mine:
        copy.start()
    a_copy = pltpu.make_async_copy(a_ref, a_vmem, local_sem.at[halves])
    a_copy.start()
    for h in range(halves):
        mine[h].wait()
        s_copy(0, h).start()

    a_copy.wait()
    tile = 64

    def split_a(k, index, carry):
        rows = pl.ds(pl.multiple_of(index * tile, tile), tile)
        owner = lax.rem(me + (rep - 1) * STEPS + k + n, n)
        parts = [a_vmem[k * A_SLOTS + m, rows, :] for m in range(A_SLOTS)]
        for i in range(ROWS_DEV):
            for j in range(ROWS_DEV):
                total = None
                for m in range(A_SLOTS):
                    g = k * A_SLOTS + m
                    match = (a_rows[0, g] == me * ROWS_DEV + i) & (
                        a_cols[0, g] == owner * ROWS_DEV + j
                    )
                    term = jnp.where(match, 1.0, 0.0).astype(jnp.float32) * parts[m]
                    total = term if total is None else total + term
                high = total.astype(jnp.bfloat16)
                low = (total - high.astype(jnp.float32)).astype(jnp.bfloat16)
                a_split[k, j, i, rows, pl.ds(0, block)] = high
                a_split[k, j, i, rows, pl.ds(block, block)] = low
                a_split[k, j, i, rows, pl.ds(2 * block, block)] = high
        return carry

    for k in range(STEPS):
        lax.fori_loop(0, block // tile, functools.partial(split_a, k), 0)

    def clear(index, carry):
        h = index // targets
        t = lax.rem(index, targets)
        acc[h, t] = jnp.zeros((block, LANES), jnp.float32)
        return carry

    lax.fori_loop(0, halves * targets, clear, 0)

    def fetch(first, count):
        copy = pltpu.make_async_copy(
            metas.at[:, pl.ds(first, count)],
            metas_s.at[:, pl.ds(first, count)],
            local_sem.at[halves + 1],
        )
        copy.start()
        copy.wait()

    def step_of(line, slot):
        back = STEPS - 2 * slot + line * (1 - 2 * core)
        forth = 2 * slot + line * (1 - 2 * core)
        k = jnp.where(rep == 0, back, forth)
        return k, (k >= 0) & (k < STEPS)

    def multiply(line, slot, h, k, into, q):
        piece = panels[line, slot, h, q]
        high = piece.astype(jnp.bfloat16)
        low = (piece - high.astype(jnp.float32)).astype(jnp.bfloat16)
        stacked = jnp.concatenate([high, high, low], axis=0)
        j = lax.rem(metas_s[line, slot, 0, q], ROWS_DEV)
        left = a_split[k, j].reshape(ROWS_DEV * block, 3 * block)
        product = jnp.dot(left, stacked, preferred_element_type=jnp.float32)
        prods[into, q] = product.reshape(ROWS_DEV, block, LANES)

    def multiply_if(line, slot, h, into, q):
        k, needed = step_of(line, slot)

        @pl.when(needed)
        def _():
            multiply(line, slot, h, k, into, q)

    def collect(line, slot, h, into, t):
        i = lax.rem(c_rows[0, t], ROWS_DEV)
        total = acc[h, t]
        for q in range(q_count):
            match = metas_s[line, slot, 1, q] == c_cols[0, t]
            total = total + jnp.where(match, 1.0, 0.0).astype(jnp.float32) * prods[into, q, i]
        acc[h, t] = total

    def collect_all(line, slot, h, into):
        k, needed = step_of(line, slot)

        @pl.when(needed)
        def _():
            def body(t, carry):
                collect(line, slot, h, into, t)
                return carry

            lax.fori_loop(0, targets, body, 0)

    def compute(line, slot, h):
        k, needed = step_of(line, slot)

        @pl.when(needed)
        def _():
            def body(q, carry):
                multiply(line, slot, h, k, 2, q)
                return carry

            lax.fori_loop(0, q_count, body, 0)

        collect_all(line, slot, h, 2)

    few = q_count // 3
    many = 2 * few

    for h in range(halves):
        for q in range(q_count):
            if h == 0 and q == 0:
                m_z.wait_recv()

                @pl.when(near == 1)
                def _():
                    m_xp.start()

                m_s[2].start()
            z_copy(h, q).wait_recv()

            @pl.when(near == 1)
            def _():
                x_pass(h, q).start()
                if q < few:
                    d_copy(h, q).start()

            if q < many:

                @pl.when(near == 0)
                def _():
                    p_copy(h, q).start()

            if h > 0:
                multiply_if(0, 2, h, 0, q)
            x_own(h, q).wait_recv()
            if q >= many:
                f_copy(h, q).start()
            elif q >= few:

                @pl.when(near == 0)
                def _():
                    f_copy(h, q).start()

            if h > 0:
                multiply_if(0, 1, h, 1, q)
                if q == q_count // 2:
                    compute(0, 0, h)
                    s_copy(0, h).wait_recv()
                    compute(1, 0, h)
            elif q == 0:
                m_x.wait_recv()
                m_f.start()
                m_s[1].start()
        s_copy(2, h).start()
        s_copy(1, h).start()
        if h + 1 < halves:
            start_own(h + 1)
        if h == 0:
            for s in range(slots - 1):
                m_s[s].wait_recv()
            fetch(0, slots - 1)
            compute(0, 2, h)
            compute(0, 1, h)
        else:
            collect_all(0, 2, h, 0)
            collect_all(0, 1, h, 1)
        s_copy(2, h).wait_recv()
        compute(1, 2, h)

        @pl.when(near == 1)
        def _():
            for q in range(few):
                d_copy(h, q).wait_recv()
                dp_copy(h, q).start()

        s_copy(1, h).wait_recv()
        compute(1, 1, h)
        if h == 0:
            compute(0, 0, h)
            s_copy(0, h).wait_recv()
            compute(1, 0, h)
            m_f.wait_recv()
            m_s[3].start()
            m_s[3].wait_recv()
            fetch(slots - 1, 1)
        order = list(range(few, many)) + list(range(few)) + list(range(many, q_count))
        previous = None
        for q in order:
            f_copy(h, q).wait_recv()
            t_copy(h, q).start()
            multiply_if(0, 3, h, 0, q)
            if previous is not None:
                t_copy(h, previous).wait_recv()
                multiply_if(1, 3, h, 1, previous)
            previous = q
        t_copy(h, previous).wait_recv()
        multiply_if(1, 3, h, 1, previous)

        def last(base, t):
            for line in range(2):
                k, needed = step_of(line, 3)

                @pl.when(needed)
                def _():
                    collect(line, 3, h, line, base + t)

        def theirs(u, carry):
            last((1 - rep) * keep, u)

            @pl.when(u > 0)
            def _():
                y_copy(h, u - 1).start()

            return carry

        def ours(u, carry):
            last(rep * keep, u)
            return carry

        lax.fori_loop(0, keep, theirs, 0)
        y_copy(h, keep - 1).start()
        lax.fori_loop(0, keep, ours, 0)

    for h in range(halves):

        def finish(u, carry):
            y_copy(h, u).wait_recv()
            out_ref[u, :, pl.ds(h * LANES, LANES)] = acc[h, rep * keep + u] + far[h, u]
            return carry

        lax.fori_loop(0, keep, finish, 0)

    for copy in [m_z, m_x, m_f] + m_s:
        copy.wait_send()
    for h in range(halves):
        for u in range(keep):
            y_copy(h, u).wait_send()
        for s in range(slots - 1):
            s_copy(s, h).wait_send()
        for q in range(q_count):
            z_copy(h, q).wait_send()
            x_own(h, q).wait_send()
            t_copy(h, q).wait_send()
            if q < few:
                p_copy(h, q).wait_send()

                @pl.when(near == 1)
                def _():
                    d_copy(h, q).wait_send()

            elif q < many:

                @pl.when(near == 0)
                def _():
                    p_copy(h, q).wait_send()
                    f_copy(h, q).wait_send()

            else:
                f_copy(h, q).wait_send()


def local(n, a_blocks, a_rows, a_cols, b_blocks, b_rows, b_cols, b_count, c_rows, c_cols):
    replica = lax.axis_index("rep")
    q_count, block = b_blocks.shape[1], b_blocks.shape[-1]
    a_slots = a_blocks.shape[1]
    targets = c_rows.shape[1]
    half = targets // lax.axis_size("rep")
    halves = block // LANES
    slots = STEPS // 2 + 1
    smem = pl.BlockSpec(memory_space=pltpu.SMEM)
    vmem = pl.BlockSpec(memory_space=pltpu.VMEM)
    hbm = pl.BlockSpec(memory_space=pl.ANY)
    dma = pltpu.SemaphoreType.DMA
    summed = pl.pallas_call(
        functools.partial(kernel, n),
        out_shape=jax.ShapeDtypeStruct((half, block, block), jnp.float32),
        in_specs=[smem] * 7 + [hbm, hbm],
        out_specs=vmem,
        scratch_shapes=[
            pltpu.VMEM((2, slots, halves, q_count, block, LANES), jnp.float32),
            pltpu.VMEM((halves, q_count // 3, block, LANES), jnp.float32),
            pltpu.VMEM((2, slots, 8, LANES), jnp.int32),
            pltpu.SMEM((2, slots, 8, LANES), jnp.int32),
            pltpu.VMEM((a_slots, block, block), jnp.float32),
            pltpu.VMEM((STEPS, ROWS_DEV, ROWS_DEV, block, 3 * block), jnp.bfloat16),
            pltpu.VMEM((3, q_count, ROWS_DEV, block, LANES), jnp.float32),
            pltpu.VMEM((halves, targets, block, LANES), jnp.float32),
            pltpu.VMEM((halves, half, block, LANES), jnp.float32),
            dma((halves + 2,)),
            dma((halves, q_count)),
            dma((halves, q_count)),
            dma((halves, q_count)),
            dma((halves, q_count)),
            dma((halves, q_count)),
            dma((halves, q_count)),
            dma((slots, halves)),
            dma((slots, halves)),
            dma((halves, q_count)),
            dma((halves, q_count)),
            dma((halves, q_count)),
            dma((halves, q_count)),
            dma((halves, half)),
            dma((halves, half)),
            dma((3 + slots,)),
            dma((3 + slots,)),
        ],
        compiler_params=pltpu.CompilerParams(
            collective_id=0, has_side_effects=True, vmem_limit_bytes=60 * 1024 * 1024
        ),
    )(a_rows, a_cols, c_rows, c_cols, b_rows, b_cols, b_count, a_blocks[0], b_blocks[0])
    rows_half = lax.dynamic_slice_in_dim(c_rows[0], replica * half, half)
    cols_half = lax.dynamic_slice_in_dim(c_cols[0], replica * half, half)
    diagonal = (rows_half == cols_half).astype(jnp.float32)
    identity = jnp.eye(block, dtype=jnp.float32)
    result = 1.5 * diagonal[:, None, None] * identity[None, :, :] - 0.5 * summed
    return result[None]


def solution(mesh):
    return jax.shard_map(
        functools.partial(local, mesh.shape["blk"]),
        mesh=mesh,
        in_specs=(
            P("blk", "rep", None, None),
            P("blk", "rep"),
            P("blk", "rep"),
            P("blk", None, None, None),
            P("blk", None),
            P("blk", None),
            P("blk"),
            P("blk", None),
            P("blk", None),
        ),
        out_specs=P("blk", "rep", None, None),
        check_vma=False,
    )
```

```python
import functools

import jax
import jax.numpy as jnp
from jax import lax
from jax.experimental import pallas as pl
from jax.experimental.pallas import tpu as pltpu
from jax.sharding import PartitionSpec as P

STEPS = 6
A_SLOTS = 4
ROWS_DEV = 2
LANES = 128
MESH = pl.DeviceIdType.MESH


def kernel(
    n,
    a_rows,
    a_cols,
    c_rows,
    c_cols,
    b_rows,
    b_cols,
    b_count,
    a_ref,
    b_ref,
    out_ref,
    panels,
    detour,
    metas,
    metas_s,
    a_vmem,
    a_split,
    prods,
    acc,
    far,
    local_sem,
    z_send,
    z_recv,
    x_send,
    x_recv,
    f_send,
    f_recv,
    s_send,
    s_recv,
    p_send,
    d_recv,
    t_send,
    t_recv,
    y_send,
    y_recv,
    m_send,
    m_recv,
):
    rep = lax.axis_index("rep")
    me = lax.axis_index("blk")
    core = lax.rem(me, 2)
    odd = lax.rem(me // 2, 2)
    slots = panels.shape[1]
    halves = panels.shape[2]
    q_count = panels.shape[3]
    block = panels.shape[4]
    targets = acc.shape[1]
    keep = targets // 2
    ahead = lax.rem(me + 4, n)
    behind = lax.rem(me + n - 4, n)
    z_to = jnp.where(rep == 0, ahead, behind)
    x_to = me + 2 - 4 * odd
    s_to = me + 1 - 2 * core
    near = jnp.where(rep == 0, odd, 1 - odd)

    sub = lax.broadcasted_iota(jnp.int32, (8, LANES), 0)
    lane = lax.broadcasted_iota(jnp.int32, (8, LANES), 1)
    meta = jnp.zeros((8, LANES), jnp.int32)
    for q in range(q_count):
        col = jnp.where(q < b_count[0], b_cols[0, q], -1)
        meta = jnp.where((sub == 0) & (lane == q), b_rows[0, q], meta)
        meta = jnp.where((sub == 1) & (lane == q), col, meta)
    metas[0, 0] = meta

    barrier = pltpu.get_barrier_semaphore()
    for other in (ahead, behind, x_to, s_to):
        pl.semaphore_signal(barrier, inc=1, device_id=(rep, other), device_id_type=MESH)
    pl.semaphore_signal(barrier, inc=1, device_id=(1 - rep, me), device_id_type=MESH)
    pl.semaphore_wait(barrier, 5)

    def remote(src, dst, send, recv, to, r=None):
        return pltpu.make_async_remote_copy(
            src_ref=src,
            dst_ref=dst,
            send_sem=send,
            recv_sem=recv,
            device_id=(rep if r is None else r, to),
            device_id_type=MESH,
        )

    def own(h, q):
        return b_ref.at[q, :, pl.ds(h * LANES, LANES)]

    def z_copy(h, q):
        return remote(own(h, q), panels.at[0, 2, h, q], z_send.at[h, q], z_recv.at[h, q], z_to)

    def x_own(h, q):
        return remote(own(h, q), panels.at[0, 1, h, q], x_send.at[h, q], x_recv.at[h, q], x_to)

    def x_pass(h, q):
        return remote(
            panels.at[0, 2, h, q], panels.at[0, 1, h, q], x_send.at[h, q], x_recv.at[h, q], x_to
        )

    def f_copy(h, q):
        return remote(
            panels.at[0, 1, h, q], panels.at[0, 3, h, q], f_send.at[h, q], f_recv.at[h, q], z_to
        )

    def p_copy(h, q):
        return remote(
            panels.at[0, 2, h, q], panels.at[0, 3, h, q], p_send.at[h, q], f_recv.at[h, q], x_to
        )

    def d_copy(h, q):
        return remote(
            panels.at[0, 2, h, q], detour.at[h, q], f_send.at[h, q], d_recv.at[h, q], z_to
        )

    def dp_copy(h, q):
        return remote(
            detour.at[h, q], panels.at[0, 3, h, q], p_send.at[h, q], f_recv.at[h, q], x_to
        )

    def t_copy(h, q):
        return remote(
            panels.at[0, 3, h, q], panels.at[1, 3, h, q], t_send.at[h, q], t_recv.at[h, q], s_to
        )

    def s_copy(s, h):
        return remote(panels.at[0, s, h], panels.at[1, s, h], s_send.at[s, h], s_recv.at[s, h], s_to)

    def meta_copy(index, src, line, slot, to):
        return remote(src, metas.at[line, slot], m_send.at[index], m_recv.at[index], to)

    def y_copy(h, u):
        return remote(
            acc.at[h, (1 - rep) * keep + u],
            far.at[h, u],
            y_send.at[h, u],
            y_recv.at[h, u],
            me,
            1 - rep,
        )

    def start_own(h):
        for q in range(q_count):
            z_copy(h, q).start()

        @pl.when(near == 0)
        def _():
            for q in range(q_count):
                x_own(h, q).start()

    m_z = meta_copy(0, metas.at[0, 0], 0, 2, z_to)
    m_x = meta_copy(1, metas.at[0, 0], 0, 1, x_to)
    m_xp = meta_copy(1, metas.at[0, 2], 0, 1, x_to)
    m_f = meta_copy(2, metas.at[0, 1], 0, 3, z_to)
    m_s = [meta_copy(3 + s, metas.at[0, s], 1, s, s_to) for s in range(slots)]

    m_z.start()

    @pl.when(near == 0)
    def _():
        m_x.start()

    m_s[0].start()
    start_own(0)
    mine = [
        pltpu.make_async_copy(
            b_ref.at[:, :, pl.ds(h * LANES, LANES)], panels.at[0, 0, h], local_sem.at[h]
        )
        for h in range(halves)
    ]
    for copy in mine:
        copy.start()
    a_copy = pltpu.make_async_copy(a_ref, a_vmem, local_sem.at[halves])
    a_copy.start()
    for h in range(halves):
        mine[h].wait()
        s_copy(0, h).start()

    a_copy.wait()
    tile = 64

    def split_a(k, index, carry):
        rows = pl.ds(pl.multiple_of(index * tile, tile), tile)
        owner = lax.rem(me + (rep - 1) * STEPS + k + n, n)
        parts = [a_vmem[k * A_SLOTS + m, rows, :] for m in range(A_SLOTS)]
        for i in range(ROWS_DEV):
            for j in range(ROWS_DEV):
                total = None
                for m in range(A_SLOTS):
                    g = k * A_SLOTS + m
                    match = (a_rows[0, g] == me * ROWS_DEV + i) & (
                        a_cols[0, g] == owner * ROWS_DEV + j
                    )
                    term = jnp.where(match, 1.0, 0.0).astype(jnp.float32) * parts[m]
                    total = term if total is None else total + term
                high = total.astype(jnp.bfloat16)
                low = (total - high.astype(jnp.float32)).astype(jnp.bfloat16)
                a_split[k, j, i, rows, pl.ds(0, block)] = high
                a_split[k, j, i, rows, pl.ds(block, block)] = low
                a_split[k, j, i, rows, pl.ds(2 * block, block)] = high
        return carry

    for k in range(STEPS):
        lax.fori_loop(0, block // tile, functools.partial(split_a, k), 0)

    def clear(index, carry):
        h = index // targets
        t = lax.rem(index, targets)
        acc[h, t] = jnp.zeros((block, LANES), jnp.float32)
        return carry

    lax.fori_loop(0, halves * targets, clear, 0)

    def fetch(first, count):
        copy = pltpu.make_async_copy(
            metas.at[:, pl.ds(first, count)],
            metas_s.at[:, pl.ds(first, count)],
            local_sem.at[halves + 1],
        )
        copy.start()
        copy.wait()

    def step_of(line, slot):
        back = STEPS - 2 * slot + line * (1 - 2 * core)
        forth = 2 * slot + line * (1 - 2 * core)
        k = jnp.where(rep == 0, back, forth)
        return k, (k >= 0) & (k < STEPS)

    def multiply(line, slot, h, k, into, q):
        piece = panels[line, slot, h, q]
        high = piece.astype(jnp.bfloat16)
        low = (piece - high.astype(jnp.float32)).astype(jnp.bfloat16)
        stacked = jnp.concatenate([high, high, low], axis=0)
        j = lax.rem(metas_s[line, slot, 0, q], ROWS_DEV)
        left = a_split[k, j].reshape(ROWS_DEV * block, 3 * block)
        product = jnp.dot(left, stacked, preferred_element_type=jnp.float32)
        prods[into, q] = product.reshape(ROWS_DEV, block, LANES)

    def multiply_if(line, slot, h, into, q):
        k, needed = step_of(line, slot)

        @pl.when(needed)
        def _():
            multiply(line, slot, h, k, into, q)

    def collect(line, slot, h, into, t):
        i = lax.rem(c_rows[0, t], ROWS_DEV)
        total = acc[h, t]
        for q in range(q_count):
            match = metas_s[line, slot, 1, q] == c_cols[0, t]
            total = total + jnp.where(match, 1.0, 0.0).astype(jnp.float32) * prods[into, q, i]
        acc[h, t] = total

    def collect_all(line, slot, h, into):
        k, needed = step_of(line, slot)

        @pl.when(needed)
        def _():
            def body(t, carry):
                collect(line, slot, h, into, t)
                return carry

            lax.fori_loop(0, targets, body, 0)

    def compute(line, slot, h):
        k, needed = step_of(line, slot)

        @pl.when(needed)
        def _():
            def body(q, carry):
                multiply(line, slot, h, k, 2, q)
                return carry

            lax.fori_loop(0, q_count, body, 0)

        collect_all(line, slot, h, 2)

    few = q_count // 3
    many = 2 * few

    for h in range(halves):
        for q in range(q_count):
            if h == 0 and q == 0:
                m_z.wait_recv()

                @pl.when(near == 1)
                def _():
                    m_xp.start()

                m_s[2].start()
            z_copy(h, q).wait_recv()

            @pl.when(near == 1)
            def _():
                x_pass(h, q).start()
                if q < few:
                    d_copy(h, q).start()

            if q < many:

                @pl.when(near == 0)
                def _():
                    p_copy(h, q).start()

            if h > 0:
                multiply_if(0, 2, h, 0, q)
            x_own(h, q).wait_recv()
            if q >= many:
                f_copy(h, q).start()
            elif q >= few:

                @pl.when(near == 0)
                def _():
                    f_copy(h, q).start()

            if h > 0:
                multiply_if(0, 1, h, 1, q)
                if q == q_count - 1:
                    compute(0, 0, h)
                    s_copy(0, h).wait_recv()
                    compute(1, 0, h)
            elif q == 0:
                m_x.wait_recv()
                m_f.start()
                m_s[1].start()
        s_copy(2, h).start()
        s_copy(1, h).start()
        if h + 1 < halves:
            start_own(h + 1)
        if h == 0:
            for s in range(slots - 1):
                m_s[s].wait_recv()
            fetch(0, slots - 1)
            compute(0, 2, h)
            compute(0, 1, h)
        else:
            collect_all(0, 2, h, 0)
            collect_all(0, 1, h, 1)
        s_copy(2, h).wait_recv()
        compute(1, 2, h)

        @pl.when(near == 1)
        def _():
            for q in range(few):
                d_copy(h, q).wait_recv()
                dp_copy(h, q).start()

        s_copy(1, h).wait_recv()
        compute(1, 1, h)
        if h == 0:
            compute(0, 0, h)
            s_copy(0, h).wait_recv()
            compute(1, 0, h)
            m_f.wait_recv()
            m_s[3].start()
            m_s[3].wait_recv()
            fetch(slots - 1, 1)
        order = list(range(few, many)) + list(range(few)) + list(range(many, q_count))
        previous = None
        for q in order:
            f_copy(h, q).wait_recv()
            t_copy(h, q).start()
            multiply_if(0, 3, h, 0, q)
            if previous is not None:
                t_copy(h, previous).wait_recv()
                multiply_if(1, 3, h, 1, previous)
            previous = q
        t_copy(h, previous).wait_recv()
        multiply_if(1, 3, h, 1, previous)

        def last(base, t):
            for line in range(2):
                k, needed = step_of(line, 3)

                @pl.when(needed)
                def _():
                    collect(line, 3, h, line, base + t)

        def theirs(u, carry):
            last((1 - rep) * keep, u)

            @pl.when(u > 0)
            def _():
                y_copy(h, u - 1).start()

            return carry

        def ours(u, carry):
            last(rep * keep, u)
            return carry

        lax.fori_loop(0, keep, theirs, 0)
        y_copy(h, keep - 1).start()
        lax.fori_loop(0, keep, ours, 0)

    for h in range(halves):

        def finish(u, carry):
            y_copy(h, u).wait_recv()
            out_ref[u, :, pl.ds(h * LANES, LANES)] = acc[h, rep * keep + u] + far[h, u]
            return carry

        lax.fori_loop(0, keep, finish, 0)

    for copy in [m_z, m_x, m_f] + m_s:
        copy.wait_send()
    for h in range(halves):
        for u in range(keep):
            y_copy(h, u).wait_send()
        for s in range(slots - 1):
            s_copy(s, h).wait_send()
        for q in range(q_count):
            z_copy(h, q).wait_send()
            x_own(h, q).wait_send()
            t_copy(h, q).wait_send()
            if q < few:
                p_copy(h, q).wait_send()

                @pl.when(near == 1)
                def _():
                    d_copy(h, q).wait_send()

            elif q < many:

                @pl.when(near == 0)
                def _():
                    p_copy(h, q).wait_send()
                    f_copy(h, q).wait_send()

            else:
                f_copy(h, q).wait_send()


def local(n, a_blocks, a_rows, a_cols, b_blocks, b_rows, b_cols, b_count, c_rows, c_cols):
    replica = lax.axis_index("rep")
    q_count, block = b_blocks.shape[1], b_blocks.shape[-1]
    a_slots = a_blocks.shape[1]
    targets = c_rows.shape[1]
    half = targets // lax.axis_size("rep")
    halves = block // LANES
    slots = STEPS // 2 + 1
    smem = pl.BlockSpec(memory_space=pltpu.SMEM)
    vmem = pl.BlockSpec(memory_space=pltpu.VMEM)
    hbm = pl.BlockSpec(memory_space=pl.ANY)
    dma = pltpu.SemaphoreType.DMA
    summed = pl.pallas_call(
        functools.partial(kernel, n),
        out_shape=jax.ShapeDtypeStruct((half, block, block), jnp.float32),
        in_specs=[smem] * 7 + [hbm, hbm],
        out_specs=vmem,
        scratch_shapes=[
            pltpu.VMEM((2, slots, halves, q_count, block, LANES), jnp.float32),
            pltpu.VMEM((halves, q_count // 3, block, LANES), jnp.float32),
            pltpu.VMEM((2, slots, 8, LANES), jnp.int32),
            pltpu.SMEM((2, slots, 8, LANES), jnp.int32),
            pltpu.VMEM((a_slots, block, block), jnp.float32),
            pltpu.VMEM((STEPS, ROWS_DEV, ROWS_DEV, block, 3 * block), jnp.bfloat16),
            pltpu.VMEM((3, q_count, ROWS_DEV, block, LANES), jnp.float32),
            pltpu.VMEM((halves, targets, block, LANES), jnp.float32),
            pltpu.VMEM((halves, half, block, LANES), jnp.float32),
            dma((halves + 2,)),
            dma((halves, q_count)),
            dma((halves, q_count)),
            dma((halves, q_count)),
            dma((halves, q_count)),
            dma((halves, q_count)),
            dma((halves, q_count)),
            dma((slots, halves)),
            dma((slots, halves)),
            dma((halves, q_count)),
            dma((halves, q_count)),
            dma((halves, q_count)),
            dma((halves, q_count)),
            dma((halves, half)),
            dma((halves, half)),
            dma((3 + slots,)),
            dma((3 + slots,)),
        ],
        compiler_params=pltpu.CompilerParams(
            collective_id=0, has_side_effects=True, vmem_limit_bytes=60 * 1024 * 1024
        ),
    )(a_rows, a_cols, c_rows, c_cols, b_rows, b_cols, b_count, a_blocks[0], b_blocks[0])
    rows_half = lax.dynamic_slice_in_dim(c_rows[0], replica * half, half)
    cols_half = lax.dynamic_slice_in_dim(c_cols[0], replica * half, half)
    diagonal = (rows_half == cols_half).astype(jnp.float32)
    identity = jnp.eye(block, dtype=jnp.float32)
    result = 1.5 * diagonal[:, None, None] * identity[None, :, :] - 0.5 * summed
    return result[None]


def solution(mesh):
    return jax.shard_map(
        functools.partial(local, mesh.shape["blk"]),
        mesh=mesh,
        in_specs=(
            P("blk", "rep", None, None),
            P("blk", "rep"),
            P("blk", "rep"),
            P("blk", None, None, None),
            P("blk", None),
            P("blk", None),
            P("blk"),
            P("blk", None),
            P("blk", None),
        ),
        out_specs=P("blk", "rep", None, None),
        check_vma=False,
    )
```
